256 devices in a mesh: mp: 32 (over z, y_hi, core), dp: 8 (over x, y_lo).
Axes of the slice: x: 4, y: 4 (y_hi: 2, y_lo: 2; y = y_hi * 2 + y_lo), z: 8, core: 2. Of those that a mesh axis runs over, the one named last changes fastest.
Arguments:
- tokens: bfloat16 [1024, 8192], P('mp', 'dp'), may hold values from -6 to 6
- gate_weight: bfloat16 [8192, 16384], P('dp', 'mp'), may hold values from -0.0625 to 0.0625
- up_weight: bfloat16 [8192, 16384], P('dp', 'mp'), may hold values from -0.0625 to 0.0625
- down_weight: bfloat16 [16384, 8192], P('mp', 'dp'), may hold values from -0.046875 to 0.046875
- cotangent: bfloat16 [1024, 8192], P('mp', 'dp'), may hold values from -6 to 6
Outputs:
- mixed: bfloat16 [1024, 8192], P('mp', 'dp')
- token_grad: bfloat16 [1024, 8192], P('mp', 'dp')
- gate_grad: bfloat16 [8192, 16384], P('dp', 'mp')
- up_grad: bfloat16 [8192, 16384], P('dp', 'mp')
- down_grad: bfloat16 [16384, 8192], P('mp', 'dp')
The draws below stay inside these ranges and needn't reach their ends.
All inputs are finite; a program needn't handle non-finite values.
Results may differ from the reference program's by a relative error of at most 0.005.
Values may be sent and summed in bfloat16 or wider, within the bound.
No kernel may reach another device: no remote copies, remote signals or barrier semaphores. Data moves between devices by JAX's collectives and lax.ppermute only.
A program may use at most 64 MiB of HBM per device.

```python
import jax
import jax.numpy as jnp

D = 8192
FF = 16384
TOKENS = 1024


def level_of(stream_key, extent, split, least, high):
    level, own = 1.0, jax.random.fold_in(stream_key, 6)
    for dim, parts in split:
        draws = jnp.exp(jax.random.uniform(jax.random.fold_in(own, dim), (parts,), jnp.float32, least / len(split), high / len(split)))
        level = level * jnp.repeat(draws, extent[dim] // parts).reshape([-1 if axis == dim else 1 for axis in range(len(extent))])
    return level


def scatter_about(rng, shape, spread, limit, shards=(), kind=jnp.bfloat16):
    drawn = jax.random.normal(rng, shape, jnp.float32) * spread
    if len(shards) > 0:
        drawn = level_of(rng, shape, shards, -0.22, 0.18) * drawn
    return jnp.clip(drawn, min=-limit, max=limit).astype(kind)


def setup_inputs(seed: int = 0) -> dict:
    arg_keys = jax.random.split(jax.random.key(seed), 6)
    tokens = scatter_about(arg_keys[0], (TOKENS, D), 1.0, 6.0, ((0, 32), (1, 8)))
    gate_weight = scatter_about(arg_keys[1], (D, FF), D ** -0.5, 0.0625, ((0, 8), (1, 32)))
    up_weight = scatter_about(arg_keys[2], (D, FF), D ** -0.5, 0.0625, ((0, 8), (1, 32)))
    down_weight = scatter_about(arg_keys[3], (FF, D), FF ** -0.5, 0.046875, ((0, 32), (1, 8)))
    cotangent = scatter_about(arg_keys[4], (TOKENS, D), 1.0, 6.0, ((0, 32), (1, 8)))
    return dict(tokens=tokens, gate_weight=gate_weight, up_weight=up_weight, down_weight=down_weight, cotangent=cotangent)


def reference(tokens, gate_weight, up_weight, down_weight, cotangent):
    gate = jnp.dot(tokens, gate_weight, preferred_element_type=jnp.float32)
    up = jnp.dot(tokens, up_weight, preferred_element_type=jnp.float32)
    sig = jax.nn.sigmoid(gate)
    act = gate * sig
    hidden = (act * up).astype(jnp.bfloat16)
    mixed = jnp.dot(hidden, down_weight, preferred_element_type=jnp.float32).astype(jnp.bfloat16)
    hidden_back = jnp.dot(cotangent, down_weight.T, preferred_element_type=jnp.float32)
    down_grad = jnp.dot(hidden.T, cotangent, preferred_element_type=jnp.float32).astype(jnp.bfloat16)
    pre_gate = (hidden_back * up * sig * (1.0 + gate * (1.0 - sig))).astype(jnp.bfloat16)
    pre_up = (hidden_back * act).astype(jnp.bfloat16)
    gate_grad = jnp.dot(tokens.T, pre_gate, preferred_element_type=jnp.float32).astype(jnp.bfloat16)
    up_grad = jnp.dot(tokens.T, pre_up, preferred_element_type=jnp.float32).astype(jnp.bfloat16)
    token_grad = jnp.dot(pre_gate, gate_weight.T, preferred_element_type=jnp.float32)
    token_grad = token_grad + jnp.dot(pre_up, up_weight.T, preferred_element_type=jnp.float32)
    return mixed, token_grad.astype(jnp.bfloat16), gate_grad, up_grad, down_grad
```

```python
import jax
import jax.numpy as jnp
from jax import lax
from jax.sharding import Mesh, PartitionSpec as P


f32 = jnp.float32
bf16 = jnp.bfloat16

SWAP = [(0, 1), (1, 0)]
Z_ORDER = (0, -1, 1, -2, -3, 2, 3, 4)
PEERS = ((2, 1), (2, 0), (1, 1), (3, 1), (1, 0), (3, 0), (0, 1))
DP = ("x", "yl")


def shift(value, axis, by, size):
    return lax.ppermute(value, axis, [(i, (i + by) % size) for i in range(size)])


def to_peer(value, peer):
    dx, dy = peer
    pairs = [(2 * x + y, 2 * ((x + dx) % 4) + (y ^ dy)) for x in range(4) for y in range(2)]
    return lax.ppermute(value, DP, pairs)


def dot(left, right):
    return jnp.dot(left, right, preferred_element_type=f32)


def dot_rows(left, right):
    return lax.dot_general(left, right, (((0,), (0,)), ((), ())), preferred_element_type=f32)


def dot_cols(left, right):
    return lax.dot_general(left, right, (((1,), (1,)), ((), ())), preferred_element_type=f32)


def gather_mp(own):
    before, after = shift(own, "z", 1, 8), shift(own, "z", -1, 8)
    low = jnp.concatenate([own, before], axis=0)
    high = jnp.concatenate([own, after], axis=0)
    far = shift(own, "z", 4, 8)
    low2, high2 = shift(low, "z", 2, 8), shift(high, "z", -2, 8)
    quarter = jnp.concatenate([low, after, low2, high2, far], axis=0)
    half = jnp.concatenate([quarter, lax.ppermute(quarter, "yh", SWAP)], axis=0)
    return jnp.concatenate([half, lax.ppermute(half, "core", SWAP)], axis=0)


def scatter_mp(partial):
    mine, other = partial[:512], partial[512:]
    total = mine + lax.ppermute(other.astype(bf16), "core", SWAP).astype(f32)
    mine, other = total[:256], total[256:]
    total = mine + lax.ppermute(other.astype(bf16), "yh", SWAP).astype(f32)
    send = total.astype(bf16)
    out = total[:32]
    for i in (7, 4, 6, 3, 5, 1, 2):
        out = out + shift(send[32 * i : 32 * (i + 1)], "z", Z_ORDER[i], 8).astype(f32)
    return out.astype(bf16)


def scatter_dp(partial, send, index):
    total = lax.dynamic_slice_in_dim(partial, 128 * index(0, 0), 128, 0)
    for dx, dy in PEERS:
        block = lax.dynamic_slice_in_dim(send, 128 * index(dx, dy), 128, 0)
        total = total + to_peer(block, (dx, dy)).astype(f32)
    return total


def gather_dp(share, index):
    out = jnp.zeros((1024, share.shape[1]), share.dtype)
    out = lax.dynamic_update_slice_in_dim(out, share, 128 * index(0, 0), 0)
    for dx, dy in PEERS:
        out = lax.dynamic_update_slice_in_dim(out, to_peer(share, (dx, dy)), 128 * index(-dx, dy), 0)
    return out


def body(tokens, gate_weight, up_weight, down_weight, cotangent):
    x, yl = lax.axis_index("x"), lax.axis_index("yl")

    def index(dx, dy):
        return 2 * ((x + dx) % 4) + (yl ^ dy)

    width = gate_weight.shape[1]
    both_weights = jnp.concatenate([gate_weight, up_weight], axis=1)
    token_all = gather_mp(tokens)
    cot_all = gather_mp(cotangent)
    partial = dot(token_all, both_weights)
    both = scatter_dp(partial, partial.astype(bf16), index)
    partial = dot_cols(cot_all, down_weight)
    hidden_back = scatter_dp(partial, partial.astype(bf16), index)

    gate, up = both[:, :width], both[:, width:]
    sig = jax.nn.sigmoid(gate)
    act = gate * sig
    hidden = (act * up).astype(bf16)
    pre_gate = (hidden_back * up * sig * (1.0 + gate * (1.0 - sig))).astype(bf16)
    pre_up = (hidden_back * act).astype(bf16)

    hidden_all = gather_dp(hidden, index)
    pre_all = gather_dp(jnp.concatenate([pre_gate, pre_up], axis=1), index)
    mixed = scatter_mp(dot(hidden_all, down_weight))
    token_grad = scatter_mp(dot_cols(pre_all, both_weights))
    down_grad = dot_rows(hidden_all, cot_all).astype(bf16)
    gate_grad = dot_rows(token_all, pre_all[:, :width]).astype(bf16)
    up_grad = dot_rows(token_all, pre_all[:, width:]).astype(bf16)
    return (mixed, token_grad, gate_grad, up_grad, down_grad)


def solution(mesh):
    fine = Mesh(mesh.devices.reshape(8, 2, 2, 4, 2), ("z", "yh", "core", "x", "yl"))
    mp, dp = ("z", "yh", "core"), ("x", "yl")
    in_specs = (P(mp, dp), P(dp, mp), P(dp, mp), P(mp, dp), P(mp, dp))
    out_specs = (P(mp, dp), P(mp, dp), P(dp, mp), P(dp, mp), P(mp, dp))
    return jax.shard_map(body, mesh=fine, in_specs=in_specs, out_specs=out_specs, check_vma=False)
```

```python
import jax
import jax.numpy as jnp
from jax import lax
from jax.sharding import Mesh, PartitionSpec as P


f32 = jnp.float32
bf16 = jnp.bfloat16

SWAP = [(0, 1), (1, 0)]
RING = ([(0, 1), (1, 0), (2, 3), (3, 2)], [(0, 3), (3, 0), (1, 2), (2, 1)])


def swap(value, axis):
    return lax.ppermute(value, axis, SWAP)


def across(value, dim):
    if dim == "c":
        return lax.ppermute(value, "yl", SWAP)
    pairs = [(4 * c + i, 4 * c + j) for c in range(2) for i, j in RING[c if dim == "p" else 1 - c]]
    return lax.ppermute(value, ("core", "x"), pairs)


def dot(left, right):
    return jnp.dot(left, right, preferred_element_type=f32)


def dot_rows(left, right):
    return lax.dot_general(left, right, (((0,), (0,)), ((), ())), preferred_element_type=f32)


def dot_cols(left, right):
    return lax.dot_general(left, right, (((1,), (1,)), ((), ())), preferred_element_type=f32)


def along_z(value, by):
    pairs = [(2 * z + c, 2 * ((z + (by if c == 0 else -by)) % 8) + c) for z in range(8) for c in range(2)]
    return lax.ppermute(value, ("z", "core"), pairs)


def join(*parts):
    return jnp.concatenate(parts, axis=0)


def gather_mp(own, first=None):
    pair = join(own, swap(own, "core"))
    near = along_z(pair, 1)
    far = along_z(own, 4)
    pairs = along_z(join(pair, near), 2)
    quarter = join(own, near, pairs, far)
    other = swap(quarter, "yh")
    if first is not None:
        other = after(other, first)
    return join(quarter, other)


def scatter_yh(total):
    return total[:256] + swap(total[256:].astype(bf16), "yh").astype(f32)


def scatter_z(total, *first):
    pairs = after(along_z(total[96:224].astype(bf16), -2), *first).astype(f32)
    far = along_z(total[224:].astype(bf16), 4).astype(f32)
    near = along_z((total[32:96] + pairs[64:]).astype(bf16), -1).astype(f32)
    last = swap(pairs[32:64] + near[32:], "core")
    return (total[:32] + far + pairs[:32] + near[:32] + last).astype(bf16)


def after(value, *others):
    return lax.optimization_barrier((value,) + others)[0]


def rows(value, start, size):
    return lax.dynamic_slice_p.bind(value, start, jnp.int32(0), slice_sizes=(size, value.shape[1]))


def scatter_dp(left, product, bits):
    keep, size, sent = left, 512, None
    for dim in "pqc":
        size //= 2
        mine, other, _ = bits[dim]
        kind = f32 if dim == "c" else bf16
        send = product(rows(keep, other, size)).astype(kind)
        sent = send if sent is None else sent
        got = across(send, dim)
        keep = product(rows(keep, mine, size)) + got.astype(f32)
        product = lambda block: block
    return keep, sent


def gather_dp(share, bits, first=None):
    for dim in "cqp":
        other = across(share, dim)
        if first is not None and dim == "q":
            other = after(other, first)
        share = jnp.where(bits[dim][2], join(share, other), join(other, share))
    return share


def body(tokens, gate_weight, up_weight, down_weight, cotangent):
    x, core = lax.axis_index("x"), lax.axis_index("core")
    first, second = (x ^ (x >> 1)) & 1, x >> 1
    bits = {"p": jnp.where(core == 0, first, second), "q": jnp.where(core == 0, second, first), "c": lax.axis_index("yl")}
    bits = {dim: (bits[dim] * size, size - bits[dim] * size, bits[dim] == 0) for dim, size in (("p", 256), ("q", 128), ("c", 64))}
    tokens, cotangent, bits = lax.optimization_barrier((tokens, cotangent, bits))

    width = gate_weight.shape[1]
    own_weights = jnp.concatenate([gate_weight, up_weight], axis=1)
    both_weights = jnp.concatenate([own_weights, swap(own_weights, "core")], axis=1)
    down_weights = join(down_weight, swap(down_weight, "core"))

    depth = tokens.shape[1]
    token_half = gather_mp(tokens)
    both, sent = scatter_dp(token_half, lambda block: dot(block, both_weights), bits)
    cot_half = gather_mp(cotangent, sent)
    hidden_back, _ = scatter_dp(cot_half, lambda block: dot_cols(block, down_weights), bits)

    gate = jnp.concatenate([both[:, :width], both[:, 2 * width : 3 * width]], axis=1)
    up = jnp.concatenate([both[:, width : 2 * width], both[:, 3 * width :]], axis=1)
    hidden = (gate * jax.nn.sigmoid(gate) * up).astype(bf16)
    hidden, gate, up = lax.optimization_barrier((hidden, gate, up))
    sig = jax.nn.sigmoid(gate)
    act = gate * sig
    pre_gate = (hidden_back * up * sig * (1.0 + gate * (1.0 - sig))).astype(bf16)
    pre_up = (hidden_back * act).astype(bf16)
    pre = jnp.concatenate(
        [pre_gate[:, :width], pre_up[:, :width], pre_gate[:, width:], pre_up[:, width:]], axis=1
    )
    hidden_half = gather_dp(hidden, bits, pre)
    pre_half = gather_dp(pre, bits)

    token_other, cot_other = swap(token_half, "core"), swap(cot_half, "core")
    hidden_other = swap(hidden_half[:, width:], "core")
    pre_other = swap(pre_half[:, 2 * width :], "core")
    down_grad = (dot_rows(hidden_half[:, :width], cot_half) + dot_rows(hidden_other, cot_other)).astype(bf16)
    grads = (dot_rows(token_half, pre_half[:, : 2 * width]) + dot_rows(token_other, pre_other)).astype(bf16)

    mixed = scatter_yh(dot(hidden_half, down_weights))
    token_grad = scatter_yh(dot_cols(pre_half, both_weights))
    out = scatter_z(jnp.concatenate([mixed, token_grad], axis=1), grads, down_grad)
    return (out[:, :depth], out[:, depth:], grads[:, :width], grads[:, width:], down_grad)


def solution(mesh):
    fine = Mesh(mesh.devices.reshape(8, 2, 2, 4, 2), ("z", "yh", "core", "x", "yl"))
    mp, dp = ("z", "yh", "core"), ("x", "yl")
    in_specs = (P(mp, dp), P(dp, mp), P(dp, mp), P(mp, dp), P(mp, dp))
    out_specs = (P(mp, dp), P(mp, dp), P(dp, mp), P(dp, mp), P(mp, dp))
    return jax.shard_map(body, mesh=fine, in_specs=in_specs, out_specs=out_specs, check_vma=False)
```

```python
import jax
import jax.numpy as jnp
from jax import lax
from jax.sharding import Mesh, PartitionSpec as P


f32 = jnp.float32
bf16 = jnp.bfloat16

SWAP = [(0, 1), (1, 0)]
RING = ([(0, 1), (1, 0), (2, 3), (3, 2)], [(0, 3), (3, 0), (1, 2), (2, 1)])


def swap(value, axis):
    return lax.ppermute(value, axis, SWAP)


def across(value, dim):
    if dim == "c":
        return lax.ppermute(value, "yl", SWAP)
    pairs = [(4 * c + i, 4 * c + j) for c in range(2) for i, j in RING[c if dim == "p" else 1 - c]]
    return lax.ppermute(value, ("core", "x"), pairs)


def dot(left, right):
    return jnp.dot(left, right, preferred_element_type=f32)


def dot_rows(left, right):
    return lax.dot_general(left, right, (((0,), (0,)), ((), ())), preferred_element_type=f32)


def dot_cols(left, right):
    return lax.dot_general(left, right, (((1,), (1,)), ((), ())), preferred_element_type=f32)


def along_z(value, by):
    pairs = [(2 * z + c, 2 * ((z + (by if c == 0 else -by)) % 8) + c) for z in range(8) for c in range(2)]
    return lax.ppermute(value, ("z", "core"), pairs)


def join(*parts):
    return jnp.concatenate(parts, axis=0)


def gather_mp(own, first=None):
    pair = join(own, swap(own, "core"))
    near = along_z(pair, 1)
    far = along_z(own, 4)
    pairs = along_z(join(pair, near), 2)
    quarter = join(own, near, pairs, far)
    other = swap(quarter, "yh")
    if first is not None:
        other = after(other, first)
    return join(quarter, other)


def scatter_yh(total):
    return total[:256] + swap(total[256:].astype(bf16), "yh").astype(f32)


def scatter_z(total, *first):
    pairs = after(along_z(total[96:224].astype(bf16), -2), *first).astype(f32)
    far = along_z(total[224:].astype(bf16), 4).astype(f32)
    near = along_z((total[32:96] + pairs[64:]).astype(bf16), -1).astype(f32)
    last = swap(pairs[32:64] + near[32:], "core")
    return (total[:32] + far + pairs[:32] + near[:32] + last).astype(bf16)


def after(value, *others):
    return lax.optimization_barrier((value,) + others)[0]


def rows(value, start, size):
    return lax.dynamic_slice_p.bind(value, start, jnp.int32(0), slice_sizes=(size, value.shape[1]))


def scatter_dp(left, product, bits):
    keep, size, sent = left, 512, None
    for dim in "pqc":
        size //= 2
        mine, other, _ = bits[dim]
        kind = f32 if dim == "c" else bf16
        send = product(rows(keep, other, size)).astype(kind)
        sent = send if sent is None else sent
        got = across(send, dim)
        keep = product(rows(keep, mine, size)) + got.astype(f32)
        product = lambda block: block
    return keep, sent


def gather_dp(share, bits, **first):
    for dim in "cqp":
        last = share
        other = across(share, dim)
        if dim in first:
            other = after(other, first[dim])
        share = jnp.where(bits[dim][2], join(share, other), join(other, share))
    return share, last


def body(tokens, gate_weight, up_weight, down_weight, cotangent):
    x, core = lax.axis_index("x"), lax.axis_index("core")
    first, second = (x ^ (x >> 1)) & 1, x >> 1
    bits = {"p": jnp.where(core == 0, first, second), "q": jnp.where(core == 0, second, first), "c": lax.axis_index("yl")}
    bits = {dim: (bits[dim] * size, size - bits[dim] * size, bits[dim] == 0) for dim, size in (("p", 256), ("q", 128), ("c", 64))}
    tokens, cotangent, bits = lax.optimization_barrier((tokens, cotangent, bits))

    width = gate_weight.shape[1]
    own_weights = jnp.concatenate([gate_weight, up_weight], axis=1)
    both_weights = jnp.concatenate([own_weights, swap(own_weights, "core")], axis=1)
    down_weights = join(down_weight, swap(down_weight, "core"))

    depth = tokens.shape[1]
    token_half = gather_mp(tokens)
    both, sent = scatter_dp(token_half, lambda block: dot(block, both_weights), bits)
    cot_half = gather_mp(cotangent, sent)
    hidden_back, _ = scatter_dp(cot_half, lambda block: dot_cols(block, down_weights), bits)

    gate = jnp.concatenate([both[:, :width], both[:, 2 * width : 3 * width]], axis=1)
    up = jnp.concatenate([both[:, width : 2 * width], both[:, 3 * width :]], axis=1)
    hidden = (gate * jax.nn.sigmoid(gate) * up).astype(bf16)
    hidden, gate, up = lax.optimization_barrier((hidden, gate, up))
    sig = jax.nn.sigmoid(gate)
    act = gate * sig
    pre_gate = (hidden_back * up * sig * (1.0 + gate * (1.0 - sig))).astype(bf16)
    pre_up = (hidden_back * act).astype(bf16)
    pre = jnp.concatenate(
        [pre_gate[:, :width], pre_up[:, :width], pre_gate[:, width:], pre_up[:, width:]], axis=1
    )
    pre_half, last = gather_dp(pre, bits)
    hidden_half, _ = gather_dp(hidden, bits, q=pre, p=last)

    token_other, cot_other = swap(token_half, "core"), swap(cot_half, "core")
    hidden_other = swap(hidden_half[:, width:], "core")
    pre_other = swap(pre_half[:, 2 * width :], "core")
    down_grad = (dot_rows(hidden_half[:, :width], cot_half) + dot_rows(hidden_other, cot_other)).astype(bf16)
    grads = (dot_rows(token_half, pre_half[:, : 2 * width]) + dot_rows(token_other, pre_other)).astype(bf16)

    mixed = scatter_yh(dot(hidden_half, down_weights))
    token_grad = scatter_yh(dot_cols(pre_half, both_weights))
    out = scatter_z(jnp.concatenate([mixed, token_grad], axis=1), grads, down_grad)
    return (out[:, :depth], out[:, depth:], grads[:, :width], grads[:, width:], down_grad)


def solution(mesh):
    fine = Mesh(mesh.devices.reshape(8, 2, 2, 4, 2), ("z", "yh", "core", "x", "yl"))
    mp, dp = ("z", "yh", "core"), ("x", "yl")
    in_specs = (P(mp, dp), P(dp, mp), P(dp, mp), P(mp, dp), P(mp, dp))
    out_specs = (P(mp, dp), P(mp, dp), P(dp, mp), P(dp, mp), P(mp, dp))
    return jax.shard_map(body, mesh=fine, in_specs=in_specs, out_specs=out_specs, check_vma=False)
```
